32 devices in a mesh: dp: 16 (over z, y, x), mp: 2 (over core).
Axes of the slice: x: 2, y: 2, z: 4, core: 2. Of those that a mesh axis runs over, the one named last changes fastest.
Arguments:
- tokens: bfloat16 [8192, 1024], P('dp'), may hold values from -6 to 6
- sample_owner: int32 [128], P('dp'), may hold values from 0 to 15, as said below
- sample_slot: int32 [128], P('dp'), may hold values from 0 to 15
- teacher_cache: bfloat16 [256, 64, 3200], P('dp', None, 'mp'), may hold values from -6 to 6
- fc_weight: bfloat16 [1024, 4096], P(None, 'mp'), may hold values from -0.1875 to 0.1875
- proj_weight: bfloat16 [4096, 1024], P('mp'), may hold values from -0.09375 to 0.09375
- head_weight: bfloat16 [1024, 3200], P(None, 'mp'), may hold values from -0.1875 to 0.1875
Outputs:
- fc_grad: float32 [1024, 4096], P('dp', 'mp')
- proj_grad: float32 [4096, 1024], P('mp', 'dp')
- head_grad: float32 [1024, 3200], P('dp', 'mp')
The draws below stay inside these ranges and needn't reach their ends.
Inputs may be any that keep to these rules, and one draw needn't show every extreme that they name: `sample_owner`: the 8 samples of the index d of dp name 8 different owners, among them (d - 1) mod 16 and (d + 8) mod 16; some owners are named far more often than others.
All inputs are finite; a program needn't handle non-finite values.
Results may differ from the reference program's by a relative error of at most 0.01.
Values may be sent and summed in bfloat16 or wider, within the bound.
A program may use at most 128 MiB of HBM per device.

```python
import math
import jax
import jax.numpy as jnp
from jax import lax

D = 1024
FF = 4096
FEAT = 3200
PATCH_S = 64
B_DEV = 8
CACHE_DEV = 16
SAMPLES = 128
TOKENS = 8192
CACHE = 256
N_DP = 16
N_MP = 2


def draw_sample_owner(key, part):
    devices = SAMPLES // B_DEV
    key_pop, key_jitter = jax.random.split(jax.random.fold_in(key, 11))
    popular = jax.random.randint(key_pop, (devices,), 0, 4) * 262144
    jitter = jax.random.randint(key_jitter, (devices, devices), 0, 1048576)
    scores = (popular[None, :] + jitter) * devices + jnp.arange(devices, dtype=jnp.int32)[None, :]
    rows = jnp.arange(devices, dtype=jnp.int32)[:, None]
    columns = jnp.arange(devices, dtype=jnp.int32)[None, :]
    prev_owner = (rows + devices - 1) % devices
    far_owner = (rows + devices // 2) % devices
    scores = jnp.where(columns == prev_owner, jnp.int32(1073741825), scores)
    scores = jnp.where(columns == far_owner, jnp.int32(1073741824), scores)
    _, chosen = lax.top_k(scores, B_DEV)
    return chosen.reshape(SAMPLES).astype(jnp.int32)


def place_ends(entries, key, smallest, high):
    place = [jax.random.randint(jax.random.fold_in(key, axis), (), 0, length) for axis, length in enumerate(entries.shape)]
    longest = entries.shape.index(max(entries.shape))
    next_to = place[:longest] + [(place[longest] + 1) % entries.shape[longest]] + place[longest + 1:]
    return entries.at[tuple(place)].set(smallest).at[tuple(next_to)].set(high)


def block_levels(own_key, extent, shards, least, largest):
    factor_of = 1.0
    for axis_at, shards_of in shards:
        steps = jax.random.uniform(jax.random.fold_in(jax.random.fold_in(own_key, 6), axis_at), (shards_of,), jnp.float32, least / len(shards), largest / len(shards))
        factor_of = factor_of * jnp.repeat(jnp.exp(steps), extent[axis_at] // shards_of).reshape((-1,) + (1,) * (len(extent) - 1 - axis_at))
    return factor_of


def noise(rng, dims, scale, reach, cuts=(), kind=jnp.bfloat16):
    factor_of = block_levels(rng, dims, cuts, -0.22, 0.18) if cuts else 1.0
    result = jax.random.normal(rng, dims, jnp.float32) * scale * factor_of
    return jnp.minimum(jnp.maximum(result, -reach), reach).astype(kind)


def setup_inputs(seed: int = 0) -> dict:
    arg_keys = jax.random.split(jax.random.key(seed), 8)
    tokens = noise(arg_keys[0], (TOKENS, D), 1.0, 6.0, ((0, 16),))
    sample_owner = draw_sample_owner(jax.random.fold_in(arg_keys[7], 71), 0)
    sample_slot = place_ends(jax.random.randint(arg_keys[2], (SAMPLES,), 0, CACHE_DEV), jax.random.fold_in(arg_keys[2], 1), 0, CACHE_DEV - 1).astype(jnp.int32)
    teacher_cache = noise(arg_keys[3], (CACHE, PATCH_S, FEAT), 1.0, 6.0, ((0, 16), (2, 2)))
    fc_weight = noise(arg_keys[4], (D, FF), D ** -0.5, 0.1875, ((1, 2),))
    proj_weight = noise(arg_keys[5], (FF, D), FF ** -0.5, 0.09375, ((0, 2),))
    head_weight = noise(arg_keys[6], (D, FEAT), D ** -0.5, 0.1875, ((1, 2),))
    return {"tokens": tokens, "sample_owner": sample_owner, "sample_slot": sample_slot, "teacher_cache": teacher_cache, "fc_weight": fc_weight, "proj_weight": proj_weight, "head_weight": head_weight}


gelu_coef = 0.7978845608

def normalize(values):
    values = values.astype(jnp.float32)
    center = lax.optimization_barrier(jnp.mean(values, axis=-1, keepdims=True))
    spread = lax.optimization_barrier(jnp.mean((values - center) ** 2, axis=-1, keepdims=True))
    inverse = 1.0 / jnp.sqrt(spread + 1e-06)
    return ((values - center) * inverse, inverse)

def gelu_tanh(values):
    return 0.5 * values * (1.0 + jnp.tanh(gelu_coef * (values + 0.044715 * values ** 3)))

def gelu_slope(values):
    inner = jnp.tanh(gelu_coef * (values + 0.044715 * values ** 3))
    return 0.5 * (1.0 + inner) + 0.5 * values * (1.0 - inner * inner) * gelu_coef * (1.0 + 3.0 * 0.044715 * values * values)

def rounded(values):
    lowered = lax.optimization_barrier(values.astype(jnp.bfloat16))
    return lowered.astype(jnp.float32)

def reference(tokens, sample_owner, sample_slot, teacher_cache, fc_weight, proj_weight, head_weight):
    tok_rows = B_DEV * PATCH_S
    loss_scale = 1.0 / math.sqrt(TOKENS)
    half_hidden = FF // N_MP
    half_feat = FEAT // N_MP

    def block_step(totals, inputs):
        tok_block, owner_ids, slot_ids = inputs
        block_index = (owner_ids * CACHE_DEV + slot_ids).astype(jnp.int32)
        target = jnp.take(teacher_cache, block_index, axis=0).reshape(tok_rows, FEAT)
        normal_in, _ = normalize(tok_block)
        normed_in = normal_in.astype(jnp.bfloat16)
        pre_act = jnp.dot(normed_in, fc_weight, preferred_element_type=jnp.float32)
        act_out = gelu_tanh(pre_act).astype(jnp.bfloat16)
        mlp_out = jnp.zeros((tok_rows, D), jnp.float32)
        for group in range(N_MP):
            lower = group * half_hidden
            mlp_out = mlp_out + rounded(jnp.dot(act_out[:, lower:lower + half_hidden], proj_weight[lower:lower + half_hidden], preferred_element_type=jnp.float32))
        hidden = tok_block.astype(jnp.float32) + mlp_out
        normal_out, inverse = normalize(hidden)
        normed_out = normal_out.astype(jnp.bfloat16)
        pred = jnp.dot(normed_out, head_weight, preferred_element_type=jnp.float32)
        err_scaled = ((pred - target.astype(jnp.float32)) * loss_scale).astype(jnp.bfloat16)
        head_grad = jnp.dot(normed_out.T, err_scaled, preferred_element_type=jnp.float32)
        grad_norm = jnp.zeros((tok_rows, D), jnp.float32)
        for group in range(N_MP):
            lower = group * half_feat
            grad_norm = grad_norm + rounded(jnp.dot(err_scaled[:, lower:lower + half_feat], head_weight[:, lower:lower + half_feat].T, preferred_element_type=jnp.float32))
        grad_hidden = inverse * (grad_norm - lax.optimization_barrier(jnp.mean(grad_norm, axis=-1, keepdims=True)) - normal_out * lax.optimization_barrier(jnp.mean(grad_norm * normal_out, axis=-1, keepdims=True)))
        grad_hidden = grad_hidden.astype(jnp.bfloat16)
        proj_grad = jnp.dot(act_out.T, grad_hidden, preferred_element_type=jnp.float32)
        grad_act = jnp.dot(grad_hidden, proj_weight.T, preferred_element_type=jnp.float32)
        grad_pre = (grad_act * gelu_slope(pre_act)).astype(jnp.bfloat16)
        fc_grad = jnp.dot(normed_in.T, grad_pre, preferred_element_type=jnp.float32)
        return ((totals[0] + fc_grad, totals[1] + proj_grad, totals[2] + head_grad), None)
    start = (jnp.zeros((D, FF), jnp.float32), jnp.zeros((FF, D), jnp.float32), jnp.zeros((D, FEAT), jnp.float32))
    inputs = (tokens.reshape(N_DP, tok_rows, D), sample_owner.reshape(N_DP, B_DEV), sample_slot.reshape(N_DP, B_DEV))
    totals, _ = lax.scan(block_step, start, inputs)
    return (totals[0], totals[1], totals[2])
```

```python
import math

import jax
import jax.numpy as jnp
from jax import lax
from jax.sharding import PartitionSpec as P

gelu_coef = 0.7978845608


def normalize(values):
    values = values.astype(jnp.float32)
    center = jnp.mean(values, axis=-1, keepdims=True)
    spread = jnp.mean((values - center) ** 2, axis=-1, keepdims=True)
    inverse = 1.0 / jnp.sqrt(spread + 1e-06)
    return ((values - center) * inverse, inverse)


def gelu_tanh(values):
    return 0.5 * values * (1.0 + jnp.tanh(gelu_coef * (values + 0.044715 * values**3)))


def gelu_slope(values):
    inner = jnp.tanh(gelu_coef * (values + 0.044715 * values**3))
    return 0.5 * (1.0 + inner) + 0.5 * values * (1.0 - inner * inner) * gelu_coef * (
        1.0 + 3.0 * 0.044715 * values * values
    )


def pair_sum(part):
    size = lax.axis_size("mp")
    total = part.astype(jnp.float32)
    for shift in range(1, size):
        moved = lax.ppermute(part, "mp", [(i, (i + shift) % size) for i in range(size)])
        total = total + moved.astype(jnp.float32)
    return total


def per_device(
    tokens, sample_owner, sample_slot, teacher_cache, fc_weight, proj_weight, head_weight
):
    devices = lax.axis_size("dp")
    tok_rows = tokens.shape[0]
    loss_scale = 1.0 / math.sqrt(tok_rows * devices)
    owner_table = (sample_owner[:, None] == jnp.arange(devices, dtype=jnp.int32)[None, :]).astype(
        jnp.int32
    )
    request = jnp.sum(owner_table * (sample_slot[:, None] + 1), axis=0)
    asked_slots = lax.all_to_all(request, "dp", split_axis=0, concat_axis=0, tiled=True)
    present = asked_slots > 0
    safe_slots = jnp.maximum(asked_slots - 1, 0)
    normal_in, _ = normalize(tokens)
    normed_in = normal_in.astype(jnp.bfloat16)
    pre_act = jnp.dot(normed_in, fc_weight, preferred_element_type=jnp.float32)
    act_out = gelu_tanh(pre_act).astype(jnp.bfloat16)
    partial_value = jnp.dot(act_out, proj_weight, preferred_element_type=jnp.float32)
    mlp_out = pair_sum(partial_value.astype(jnp.bfloat16))
    hidden = tokens.astype(jnp.float32) + mlp_out
    normal_out, inverse = normalize(hidden)
    normed_out = normal_out.astype(jnp.bfloat16)
    stored = (
        jnp.take(teacher_cache, safe_slots, axis=0) * present.astype(jnp.bfloat16)[:, None, None]
    )
    arrived = lax.all_to_all(stored, "dp", split_axis=0, concat_axis=0, tiled=True)
    target = jnp.take(arrived, sample_owner, axis=0).reshape(tok_rows, -1)
    pred = jnp.dot(normed_out, head_weight, preferred_element_type=jnp.float32)
    err_scaled = ((pred - target.astype(jnp.float32)) * loss_scale).astype(jnp.bfloat16)
    head_grad = jnp.dot(normed_out.T, err_scaled, preferred_element_type=jnp.float32)
    grad_part = jnp.dot(err_scaled, head_weight.T, preferred_element_type=jnp.float32)
    grad_norm = pair_sum(grad_part.astype(jnp.bfloat16))
    grad_hidden = inverse * (
        grad_norm
        - jnp.mean(grad_norm, axis=-1, keepdims=True)
        - normal_out * jnp.mean(grad_norm * normal_out, axis=-1, keepdims=True)
    )
    grad_hidden = grad_hidden.astype(jnp.bfloat16)
    proj_grad = jnp.dot(act_out.T, grad_hidden, preferred_element_type=jnp.float32)
    grad_act = jnp.dot(grad_hidden, proj_weight.T, preferred_element_type=jnp.float32)
    grad_pre = (grad_act * gelu_slope(pre_act)).astype(jnp.bfloat16)
    fc_grad = jnp.dot(normed_in.T, grad_pre, preferred_element_type=jnp.float32)
    fc_shard, proj_shard, head_shard = (
        lax.psum_scatter(fc_grad.astype(jnp.bfloat16), "dp", scatter_dimension=0, tiled=True).astype(jnp.float32),
        lax.psum_scatter(proj_grad.astype(jnp.bfloat16), "dp", scatter_dimension=1, tiled=True).astype(jnp.float32),
        lax.psum_scatter(head_grad.astype(jnp.bfloat16), "dp", scatter_dimension=0, tiled=True).astype(jnp.float32),
    )
    return (fc_shard, proj_shard, head_shard)


def solution(mesh):
    in_specs = (
        P("dp", None),
        P("dp"),
        P("dp"),
        P("dp", None, "mp"),
        P(None, "mp"),
        P("mp", None),
        P(None, "mp"),
    )
    out_specs = (P("dp", "mp"), P("mp", "dp"), P("dp", "mp"))
    return jax.shard_map(
        per_device, mesh=mesh, in_specs=in_specs, out_specs=out_specs, check_vma=False
    )
```

```python
import functools
import math

import jax
import jax.numpy as jnp
from jax import lax
from jax.experimental import pallas as pl
from jax.experimental.pallas import tpu as pltpu
from jax.sharding import PartitionSpec as P

gelu_coef = 0.7978845608


def normalize(values):
    values = values.astype(jnp.float32)
    center = jnp.mean(values, axis=-1, keepdims=True)
    spread = jnp.mean((values - center) ** 2, axis=-1, keepdims=True)
    inverse = 1.0 / jnp.sqrt(spread + 1e-06)
    return ((values - center) * inverse, inverse)


def gelu_tanh(values):
    return 0.5 * values * (1.0 + jnp.tanh(gelu_coef * (values + 0.044715 * values**3)))


def gelu_slope(values):
    inner = jnp.tanh(gelu_coef * (values + 0.044715 * values**3))
    return 0.5 * (1.0 + inner) + 0.5 * values * (1.0 - inner * inner) * gelu_coef * (
        1.0 + 3.0 * 0.044715 * values * values
    )


def pair_sum(part):
    size = lax.axis_size("mp")
    total = part.astype(jnp.float32)
    for shift in range(1, size):
        moved = lax.ppermute(part, "mp", [(i, (i + shift) % size) for i in range(size)])
        total = total + moved.astype(jnp.float32)
    return total


def dp_factors(mesh):
    count = mesh.shape["dp"]
    lead = mesh.devices.reshape(count, -1)[:, 0]
    spots = [getattr(device, "coords", None) for device in lead]
    if any(spot is None for spot in spots):
        return (count,)
    sizes, stride = [], 1
    while stride < count:
        moved = [a for a in range(len(spots[0])) if spots[0][a] != spots[stride][a]]
        if len(moved) != 1:
            return (count,)
        sizes.append(len({spot[moved[0]] for spot in spots}))
        stride *= sizes[-1]
    return tuple(reversed(sizes)) if stride == count else (count,)


ROWS = 16


class Plan:
    def __init__(self, factors, shapes):
        self.factors = tuple(factors)
        self.strides = [math.prod(factors[i + 1 :]) for i in range(len(factors))]
        live = [a for a in range(len(factors)) if factors[a] > 1]
        live.sort(key=lambda a: (factors[a], -a))
        self.orders = [tuple(live)]
        if len(live) > 1:
            self.orders.append((live[1], live[0], *live[2:]))
        self.live = live
        self.chunks = []
        for array, (rows, cols) in enumerate(shapes):
            step = ROWS if rows % ROWS == 0 else rows
            for start in range(0, rows, step):
                order = self.orders[len(self.chunks) % len(self.orders)]
                self.chunks.append((array, start, step, cols, order))

    def scratch(self):
        shapes = []
        for _, _, step, cols, order in self.chunks:
            rest = list(range(len(self.factors)))
            for axis in order:
                rest.remove(axis)
                dims = tuple(self.factors[a] for a in rest)
                shapes.append(pltpu.VMEM((self.factors[axis] - 1, *dims, step, cols), jnp.bfloat16))
                shapes.append(pltpu.VMEM((*dims, step, cols), jnp.bfloat16))
        return shapes


def scatter_kernel(plan, arrays, *refs):
    grads, outs = refs[:arrays], refs[arrays : 2 * arrays]
    bufs, (own_sem, send_sem, recv_sem) = refs[2 * arrays : -3], refs[-3:]
    factors, strides = plan.factors, plan.strides
    me = lax.axis_index("dp")
    spot = [(me // strides[a]) % factors[a] for a in range(len(factors))]
    stages = len(plan.live)

    def peer(axis, hop):
        place = (spot[axis] + hop) % factors[axis]
        return place, me + (place - spot[axis]) * strides[axis]

    barrier = pltpu.get_barrier_semaphore()
    total = 0
    for axis in plan.live:
        for hop in range(1, factors[axis]):
            pl.semaphore_signal(
                barrier,
                inc=1,
                device_id={"dp": peer(axis, hop)[1]},
                device_id_type=pl.DeviceIdType.MESH,
            )
            total += 1
    pl.semaphore_wait(barrier, total)

    base = {axis: 0 for axis in plan.live}
    count = 0
    for axis in plan.live:
        base[axis] = count
        count += factors[axis] - 1

    def view(chunk, stage, place):
        array, start, step, _, order = plan.chunks[chunk]
        axis = order[stage]
        rest = [a for a in range(len(factors)) if a not in order[:stage]]
        index = tuple(place if a == axis else slice(None) for a in rest)
        if stage == 0:
            return grads[array].at[(*index, pl.ds(start, step))]
        return buf(chunk, stage - 1)[1].at[index]

    def buf(chunk, stage):
        at = 2 * (chunk * stages + stage)
        return bufs[at], bufs[at + 1]

    def own_copy(chunk):
        axis = plan.chunks[chunk][4][0]
        return pltpu.make_async_copy(
            view(chunk, 0, spot[axis]), buf(chunk, 0)[1], own_sem.at[chunk]
        )

    def sends(chunk, stage):
        axis = plan.chunks[chunk][4][stage]
        made = []
        for hop in range(1, factors[axis]):
            place, device = peer(axis, hop)
            made.append(
                pltpu.make_async_remote_copy(
                    src_ref=view(chunk, stage, place),
                    dst_ref=buf(chunk, stage)[0].at[hop - 1],
                    send_sem=send_sem.at[chunk, base[axis] + hop - 1],
                    recv_sem=recv_sem.at[chunk, base[axis] + hop - 1],
                    device_id={"dp": device},
                    device_id_type=pl.DeviceIdType.MESH,
                )
            )
        return made

    def launch(chunk, stage):
        for copy in sends(chunk, stage):
            copy.start()
        if stage == 0:
            own_copy(chunk).start()

    def finish(chunk, stage):
        array, start, step, _, order = plan.chunks[chunk]
        axis = order[stage]
        arrived, kept = buf(chunk, stage)
        if stage == 0:
            own_copy(chunk).wait()
        for copy in sends(chunk, stage):
            copy.wait_recv()
        rest = [a for a in range(len(factors)) if a not in order[: stage + 1]]
        dims = [factors[a] for a in rest]

        def add(flat, carry):
            at, left = [], flat
            for size in reversed(dims):
                at.insert(0, left % size)
                left = left // size
            at = tuple(at)
            if stage == 0:
                value = kept[at].astype(jnp.float32) if at else kept[...].astype(jnp.float32)
            else:
                mine, inner = buf(chunk, stage - 1)[1], list(at)
                before = [a for a in range(len(factors)) if a not in order[:stage]]
                inner.insert(before.index(axis), spot[axis])
                value = mine[tuple(inner)].astype(jnp.float32)
            for hop in range(1, factors[axis]):
                value = value + arrived[(hop - 1, *at)].astype(jnp.float32)
            if stage == stages - 1:
                outs[array][pl.ds(start, step), :] = value.reshape(step, -1)
            elif at:
                kept[at] = value.astype(jnp.bfloat16)
            return carry

        blocks = math.prod(dims)
        if blocks == 1:
            add(0, 0)
        else:
            lax.fori_loop(0, blocks, add, 0)

    width = len(plan.orders)
    groups = [
        range(at, min(at + width, len(plan.chunks))) for at in range(0, len(plan.chunks), width)
    ]
    ahead = 2
    for group in groups[:ahead]:
        for chunk in group:
            launch(chunk, 0)
    for step in range(len(groups) + stages - 1):
        for stage in range(stages):
            if 0 <= step - stage < len(groups):
                for chunk in groups[step - stage]:
                    finish(chunk, stage)
                    if stage + 1 < stages:
                        launch(chunk, stage + 1)
                if stage == 0 and step + ahead < len(groups):
                    for chunk in groups[step + ahead]:
                        launch(chunk, 0)
    for chunk in range(len(plan.chunks)):
        for stage in range(stages):
            for copy in sends(chunk, stage):
                copy.wait_send()


def scatter_sum(factors, grads):
    count = math.prod(factors)
    shapes = [(g.shape[0] // count, g.shape[1]) for g in grads]
    plan = Plan(factors, shapes)
    hops = sum(factors[a] - 1 for a in plan.live)
    chunks = len(plan.chunks)
    views = [g.reshape(*factors, *shape) for g, shape in zip(grads, shapes)]
    return pl.pallas_call(
        functools.partial(scatter_kernel, plan, len(grads)),
        out_shape=[jax.ShapeDtypeStruct(shape, jnp.float32) for shape in shapes],
        in_specs=[pl.BlockSpec(memory_space=pl.ANY)] * len(grads),
        out_specs=[pl.BlockSpec(memory_space=pltpu.VMEM)] * len(grads),
        scratch_shapes=plan.scratch()
        + [
            pltpu.SemaphoreType.DMA((chunks,)),
            pltpu.SemaphoreType.DMA((chunks, hops)),
            pltpu.SemaphoreType.DMA((chunks, hops)),
        ],
        compiler_params=pltpu.CompilerParams(
            collective_id=0, has_side_effects=True, vmem_limit_bytes=48 * 1024 * 1024
        ),
    )(*views)


def per_device(
    factors,
    tokens, sample_owner, sample_slot, teacher_cache, fc_weight, proj_weight, head_weight
):
    devices = lax.axis_size("dp")
    tok_rows = tokens.shape[0]
    loss_scale = 1.0 / math.sqrt(tok_rows * devices)
    owner_table = (sample_owner[:, None] == jnp.arange(devices, dtype=jnp.int32)[None, :]).astype(
        jnp.int32
    )
    request = jnp.sum(owner_table * (sample_slot[:, None] + 1), axis=0)
    asked_slots = lax.all_to_all(request, "dp", split_axis=0, concat_axis=0, tiled=True)
    present = asked_slots > 0
    safe_slots = jnp.maximum(asked_slots - 1, 0)
    normal_in, _ = normalize(tokens)
    normed_in = normal_in.astype(jnp.bfloat16)
    pre_act = jnp.dot(normed_in, fc_weight, preferred_element_type=jnp.float32)
    act_out = gelu_tanh(pre_act).astype(jnp.bfloat16)
    partial_value = jnp.dot(act_out, proj_weight, preferred_element_type=jnp.float32)
    mlp_out = pair_sum(partial_value.astype(jnp.bfloat16))
    hidden = tokens.astype(jnp.float32) + mlp_out
    normal_out, inverse = normalize(hidden)
    normed_out = normal_out.astype(jnp.bfloat16)
    stored = (
        jnp.take(teacher_cache, safe_slots, axis=0) * present.astype(jnp.bfloat16)[:, None, None]
    )
    arrived = lax.all_to_all(stored, "dp", split_axis=0, concat_axis=0, tiled=True)
    target = jnp.take(arrived, sample_owner, axis=0).reshape(tok_rows, -1)
    pred = jnp.dot(normed_out, head_weight, preferred_element_type=jnp.float32)
    err_scaled = ((pred - target.astype(jnp.float32)) * loss_scale).astype(jnp.bfloat16)
    head_grad = jnp.dot(normed_out.T, err_scaled, preferred_element_type=jnp.float32)
    grad_part = jnp.dot(err_scaled, head_weight.T, preferred_element_type=jnp.float32)
    grad_norm = pair_sum(grad_part.astype(jnp.bfloat16))
    grad_hidden = inverse * (
        grad_norm
        - jnp.mean(grad_norm, axis=-1, keepdims=True)
        - normal_out * jnp.mean(grad_norm * normal_out, axis=-1, keepdims=True)
    )
    grad_hidden = grad_hidden.astype(jnp.bfloat16)
    proj_grad = jnp.dot(grad_hidden.T, act_out, preferred_element_type=jnp.float32)
    grad_act = jnp.dot(grad_hidden, proj_weight.T, preferred_element_type=jnp.float32)
    grad_pre = (grad_act * gelu_slope(pre_act)).astype(jnp.bfloat16)
    fc_grad = jnp.dot(normed_in.T, grad_pre, preferred_element_type=jnp.float32)
    head_shard, proj_shard, fc_shard = scatter_sum(
        factors,
        [g.astype(jnp.bfloat16) for g in (head_grad, proj_grad, fc_grad)],
    )
    proj_shard = proj_shard.T
    return (fc_shard, proj_shard, head_shard)


def solution(mesh):
    in_specs = (
        P("dp", None),
        P("dp"),
        P("dp"),
        P("dp", None, "mp"),
        P(None, "mp"),
        P("mp", None),
        P(None, "mp"),
    )
    out_specs = (P("dp", "mp"), P("mp", "dp"), P("dp", "mp"))
    return jax.shard_map(
        functools.partial(per_device, dp_factors(mesh)),
        mesh=mesh, in_specs=in_specs, out_specs=out_specs, check_vma=False
    )
```

```python
import functools
import math

import jax
import jax.numpy as jnp
from jax import lax
from jax.experimental import pallas as pl
from jax.experimental.pallas import tpu as pltpu
from jax.sharding import PartitionSpec as P

gelu_coef = 0.7978845608


def normalize(values):
    values = values.astype(jnp.float32)
    center = jnp.mean(values, axis=-1, keepdims=True)
    spread = jnp.mean((values - center) ** 2, axis=-1, keepdims=True)
    inverse = 1.0 / jnp.sqrt(spread + 1e-06)
    return ((values - center) * inverse, inverse)


def gelu_tanh(values):
    return 0.5 * values * (1.0 + jnp.tanh(gelu_coef * (values + 0.044715 * values**3)))


def gelu_slope(values):
    inner = jnp.tanh(gelu_coef * (values + 0.044715 * values**3))
    return 0.5 * (1.0 + inner) + 0.5 * values * (1.0 - inner * inner) * gelu_coef * (
        1.0 + 3.0 * 0.044715 * values * values
    )


def pair_sum(part):
    size = lax.axis_size("mp")
    total = part.astype(jnp.float32)
    for shift in range(1, size):
        moved = lax.ppermute(part, "mp", [(i, (i + shift) % size) for i in range(size)])
        total = total + moved.astype(jnp.float32)
    return total


def dp_factors(mesh):
    count = mesh.shape["dp"]
    lead = mesh.devices.reshape(count, -1)[:, 0]
    spots = [getattr(device, "coords", None) for device in lead]
    if any(spot is None for spot in spots):
        return (count,)
    sizes, stride = [], 1
    while stride < count:
        moved = [a for a in range(len(spots[0])) if spots[0][a] != spots[stride][a]]
        if len(moved) != 1:
            return (count,)
        sizes.append(len({spot[moved[0]] for spot in spots}))
        stride *= sizes[-1]
    return tuple(reversed(sizes)) if stride == count else (count,)


ROWS = 16


class Plan:
    def __init__(self, factors, shapes):
        self.factors = tuple(factors)
        self.strides = [math.prod(factors[i + 1 :]) for i in range(len(factors))]
        live = [a for a in range(len(factors)) if factors[a] > 1]
        live.sort(key=lambda a: (factors[a], -a))
        self.orders = [tuple(live)]
        if len(live) > 1:
            self.orders.append((live[1], live[0], *live[2:]))
        self.live = live
        self.chunks = []
        early = len(live) > 2 and sum(rows // ROWS for rows, _ in shapes) > 6
        for array, (rows, cols) in enumerate(shapes):
            step = ROWS if rows % ROWS == 0 else rows
            for start in range(0, rows, step):
                order = self.orders[len(self.chunks) % len(self.orders)]
                if early and not self.chunks:
                    order = (live[2], live[1], live[0], *live[3:])
                self.chunks.append((array, start, step, cols, order))
        width, rest = len(self.orders), list(range(int(early), len(self.chunks)))
        self.groups = [rest[at : at + width] for at in range(0, len(rest), width)]
        self.early = [0] if early else []
        if early:
            self.groups[2] = [*self.groups[2], 0]

    def scratch(self):
        shapes = []
        for _, _, step, cols, order in self.chunks:
            rest = list(range(len(self.factors)))
            for axis in order:
                rest.remove(axis)
                dims = tuple(self.factors[a] for a in rest)
                shapes.append(pltpu.VMEM((self.factors[axis] - 1, *dims, step, cols), jnp.bfloat16))
                shapes.append(pltpu.VMEM((*dims, step, cols), jnp.bfloat16))
        return shapes


def scatter_kernel(plan, arrays, *refs):
    grads, outs = refs[:arrays], refs[arrays : 2 * arrays]
    bufs, (own_sem, send_sem, recv_sem) = refs[2 * arrays : -3], refs[-3:]
    factors, strides = plan.factors, plan.strides
    me = lax.axis_index("dp")
    spot = [(me // strides[a]) % factors[a] for a in range(len(factors))]
    stages = len(plan.live)

    def peer(axis, hop):
        place = (spot[axis] + hop) % factors[axis]
        return place, me + (place - spot[axis]) * strides[axis]

    barrier = pltpu.get_barrier_semaphore()
    total = 0
    for axis in plan.live:
        for hop in range(1, factors[axis]):
            pl.semaphore_signal(
                barrier,
                inc=1,
                device_id={"dp": peer(axis, hop)[1]},
                device_id_type=pl.DeviceIdType.MESH,
            )
            total += 1
    pl.semaphore_wait(barrier, total)

    base = {axis: 0 for axis in plan.live}
    count = 0
    for axis in plan.live:
        base[axis] = count
        count += factors[axis] - 1

    def view(chunk, stage, place):
        array, start, step, _, order = plan.chunks[chunk]
        axis = order[stage]
        rest = [a for a in range(len(factors)) if a not in order[:stage]]
        index = tuple(place if a == axis else slice(None) for a in rest)
        if stage == 0:
            return grads[array].at[(*index, pl.ds(start, step))]
        return buf(chunk, stage - 1)[1].at[index]

    def buf(chunk, stage):
        at = 2 * (chunk * stages + stage)
        return bufs[at], bufs[at + 1]

    def own_copy(chunk):
        axis = plan.chunks[chunk][4][0]
        return pltpu.make_async_copy(
            view(chunk, 0, spot[axis]), buf(chunk, 0)[1], own_sem.at[chunk]
        )

    def sends(chunk, stage):
        axis = plan.chunks[chunk][4][stage]
        made = []
        for hop in range(1, factors[axis]):
            place, device = peer(axis, hop)
            made.append(
                pltpu.make_async_remote_copy(
                    src_ref=view(chunk, stage, place),
                    dst_ref=buf(chunk, stage)[0].at[hop - 1],
                    send_sem=send_sem.at[chunk, base[axis] + hop - 1],
                    recv_sem=recv_sem.at[chunk, base[axis] + hop - 1],
                    device_id={"dp": device},
                    device_id_type=pl.DeviceIdType.MESH,
                )
            )
        return made

    def launch(chunk, stage):
        for copy in sends(chunk, stage):
            copy.start()
        if stage == 0:
            own_copy(chunk).start()

    def finish(chunk, stage):
        array, start, step, _, order = plan.chunks[chunk]
        axis = order[stage]
        arrived, kept = buf(chunk, stage)
        if stage == 0:
            own_copy(chunk).wait()
        for copy in sends(chunk, stage):
            copy.wait_recv()
        rest = [a for a in range(len(factors)) if a not in order[: stage + 1]]
        dims = [factors[a] for a in rest]

        def add(flat, carry):
            at, left = [], flat
            for size in reversed(dims):
                at.insert(0, left % size)
                left = left // size
            at = tuple(at)
            if stage == 0:
                value = kept[at].astype(jnp.float32) if at else kept[...].astype(jnp.float32)
            else:
                mine, inner = buf(chunk, stage - 1)[1], list(at)
                before = [a for a in range(len(factors)) if a not in order[:stage]]
                inner.insert(before.index(axis), spot[axis])
                value = mine[tuple(inner)].astype(jnp.float32)
            for hop in range(1, factors[axis]):
                value = value + arrived[(hop - 1, *at)].astype(jnp.float32)
            if stage == stages - 1:
                outs[array][pl.ds(start, step), :] = value.reshape(step, -1)
            elif at:
                kept[at] = value.astype(jnp.bfloat16)
            return carry

        blocks = math.prod(dims)
        if blocks == 1:
            add(0, 0)
        else:
            lax.fori_loop(0, blocks, add, 0)

    groups = plan.groups
    ahead = 2
    for group in [groups[0], plan.early, *groups[1:ahead]]:
        for chunk in group:
            launch(chunk, 0)
    for step in range(len(groups) + stages - 1):
        for stage in range(stages):
            if 0 <= step - stage < len(groups):
                for chunk in groups[step - stage]:
                    finish(chunk, stage)
                    if stage + 1 < stages:
                        launch(chunk, stage + 1)
                if stage == 0 and step + ahead < len(groups):
                    for chunk in groups[step + ahead]:
                        if chunk not in plan.early:
                            launch(chunk, 0)
    for chunk in range(len(plan.chunks)):
        for stage in range(stages):
            for copy in sends(chunk, stage):
                copy.wait_send()


def scatter_sum(factors, grads):
    count = math.prod(factors)
    shapes = [(g.shape[0] // count, g.shape[1]) for g in grads]
    plan = Plan(factors, shapes)
    hops = sum(factors[a] - 1 for a in plan.live)
    chunks = len(plan.chunks)
    views = [g.reshape(*factors, *shape) for g, shape in zip(grads, shapes)]
    return pl.pallas_call(
        functools.partial(scatter_kernel, plan, len(grads)),
        out_shape=[jax.ShapeDtypeStruct(shape, jnp.float32) for shape in shapes],
        in_specs=[pl.BlockSpec(memory_space=pl.ANY)] * len(grads),
        out_specs=[pl.BlockSpec(memory_space=pltpu.VMEM)] * len(grads),
        scratch_shapes=plan.scratch()
        + [
            pltpu.SemaphoreType.DMA((chunks,)),
            pltpu.SemaphoreType.DMA((chunks, hops)),
            pltpu.SemaphoreType.DMA((chunks, hops)),
        ],
        compiler_params=pltpu.CompilerParams(
            collective_id=0, has_side_effects=True, vmem_limit_bytes=48 * 1024 * 1024
        ),
    )(*views)


def error_kernel(scale, owner_ref, pred_ref, block_ref, out_ref):
    gap = pred_ref[...] - block_ref[...].astype(jnp.float32)
    out_ref[...] = (gap * scale).astype(out_ref.dtype)


def scaled_error(scale, sample_owner, pred, arrived):
    patches, width = arrived.shape[1:]
    rows = pl.BlockSpec((patches, width), lambda i, owner: (i, 0))
    picked = pl.BlockSpec((None, patches, width), lambda i, owner: (owner[i], 0, 0))
    return pl.pallas_call(
        functools.partial(error_kernel, scale),
        out_shape=jax.ShapeDtypeStruct(pred.shape, jnp.bfloat16),
        grid_spec=pltpu.PrefetchScalarGridSpec(
            num_scalar_prefetch=1,
            grid=(sample_owner.shape[0],),
            in_specs=[rows, picked],
            out_specs=rows,
        ),
        cost_estimate=pl.CostEstimate(
            flops=2 * pred.size, bytes_accessed=8 * pred.size, transcendentals=0
        ),
    )(sample_owner, pred, arrived)


def rows_kernel(left_ref, right_ref, out_ref):
    out_ref[...] = lax.dot_general(
        left_ref[...],
        right_ref[...],
        (((0,), (0,)), ((), ())),
        preferred_element_type=jnp.float32,
    ).astype(out_ref.dtype)


def outer_product(left, right):
    depth, rows = left.shape
    cols = right.shape[1]
    tile = 256 if rows % 256 == 0 else rows
    return pl.pallas_call(
        rows_kernel,
        out_shape=jax.ShapeDtypeStruct((rows, cols), jnp.bfloat16),
        grid=(rows // tile,),
        in_specs=[
            pl.BlockSpec((depth, tile), lambda i: (0, i)),
            pl.BlockSpec((depth, cols), lambda i: (0, 0)),
        ],
        out_specs=pl.BlockSpec((tile, cols), lambda i: (i, 0)),
        cost_estimate=pl.CostEstimate(
            flops=2 * depth * rows * cols,
            bytes_accessed=2 * (depth * rows + depth * cols + rows * cols),
            transcendentals=0,
        ),
    )(left, right)


def per_device(
    factors,
    tokens, sample_owner, sample_slot, teacher_cache, fc_weight, proj_weight, head_weight
):
    devices = lax.axis_size("dp")
    tok_rows = tokens.shape[0]
    loss_scale = 1.0 / math.sqrt(tok_rows * devices)
    owner_table = (sample_owner[:, None] == jnp.arange(devices, dtype=jnp.int32)[None, :]).astype(
        jnp.int32
    )
    request = jnp.sum(owner_table * (sample_slot[:, None] + 1), axis=0)
    asked_slots = lax.all_to_all(request, "dp", split_axis=0, concat_axis=0, tiled=True)
    safe_slots = jnp.maximum(asked_slots - 1, 0)
    normal_in, _ = normalize(tokens)
    normed_in = normal_in.astype(jnp.bfloat16)
    pre_act = jnp.dot(normed_in, fc_weight, preferred_element_type=jnp.float32)
    act_out = gelu_tanh(pre_act).astype(jnp.bfloat16)
    partial_value = jnp.dot(act_out, proj_weight, preferred_element_type=jnp.float32)
    mlp_out = pair_sum(partial_value.astype(jnp.bfloat16))
    hidden = tokens.astype(jnp.float32) + mlp_out
    normal_out, inverse = normalize(hidden)
    normed_out = normal_out.astype(jnp.bfloat16)
    stored = jnp.take(teacher_cache, safe_slots, axis=0, mode="clip")
    arrived = lax.all_to_all(stored, "dp", split_axis=0, concat_axis=0, tiled=True)
    pred = jnp.dot(normed_out, head_weight, preferred_element_type=jnp.float32)
    err_scaled = scaled_error(loss_scale, sample_owner, pred, arrived)
    head_grad = outer_product(normed_out, err_scaled)
    grad_part = jnp.dot(err_scaled, head_weight.T, preferred_element_type=jnp.float32)
    grad_norm = pair_sum(grad_part.astype(jnp.bfloat16))
    grad_hidden = inverse * (
        grad_norm
        - jnp.mean(grad_norm, axis=-1, keepdims=True)
        - normal_out * jnp.mean(grad_norm * normal_out, axis=-1, keepdims=True)
    )
    grad_hidden = grad_hidden.astype(jnp.bfloat16)
    proj_grad = jnp.dot(grad_hidden.T, act_out, preferred_element_type=jnp.float32)
    grad_act = jnp.dot(grad_hidden, proj_weight.T, preferred_element_type=jnp.float32)
    grad_pre = (grad_act * gelu_slope(pre_act)).astype(jnp.bfloat16)
    fc_grad = jnp.dot(normed_in.T, grad_pre, preferred_element_type=jnp.float32)
    head_shard, proj_shard, fc_shard = scatter_sum(
        factors,
        [g.astype(jnp.bfloat16) for g in (head_grad, proj_grad, fc_grad)],
    )
    proj_shard = proj_shard.T
    return (fc_shard, proj_shard, head_shard)


def solution(mesh):
    in_specs = (
        P("dp", None),
        P("dp"),
        P("dp"),
        P("dp", None, "mp"),
        P(None, "mp"),
        P("mp", None),
        P(None, "mp"),
    )
    out_specs = (P("dp", "mp"), P("mp", "dp"), P("dp", "mp"))
    return jax.shard_map(
        functools.partial(per_device, dp_factors(mesh)),
        mesh=mesh, in_specs=in_specs, out_specs=out_specs, check_vma=False
    )
```

```python
import functools
import math

import jax
import jax.numpy as jnp
from jax import lax
from jax.experimental import pallas as pl
from jax.experimental.pallas import tpu as pltpu
from jax.sharding import PartitionSpec as P

gelu_coef = 0.7978845608


def normalize(values):
    values = values.astype(jnp.float32)
    center = jnp.mean(values, axis=-1, keepdims=True)
    spread = jnp.mean((values - center) ** 2, axis=-1, keepdims=True)
    inverse = 1.0 / jnp.sqrt(spread + 1e-06)
    return ((values - center) * inverse, inverse)


def gelu_tanh(values):
    return 0.5 * values * (1.0 + jnp.tanh(gelu_coef * (values + 0.044715 * values**3)))


def gelu_slope(values):
    inner = jnp.tanh(gelu_coef * (values + 0.044715 * values**3))
    return 0.5 * (1.0 + inner) + 0.5 * values * (1.0 - inner * inner) * gelu_coef * (
        1.0 + 3.0 * 0.044715 * values * values
    )


def pair_sum(part):
    size = lax.axis_size("mp")
    total = part.astype(jnp.float32)
    for shift in range(1, size):
        moved = lax.ppermute(part, "mp", [(i, (i + shift) % size) for i in range(size)])
        total = total + moved.astype(jnp.float32)
    return total


def dp_factors(mesh):
    count = mesh.shape["dp"]
    lead = mesh.devices.reshape(count, -1)[:, 0]
    spots = [getattr(device, "coords", None) for device in lead]
    if any(spot is None for spot in spots):
        return (count,)
    sizes, stride = [], 1
    while stride < count:
        moved = [a for a in range(len(spots[0])) if spots[0][a] != spots[stride][a]]
        if len(moved) != 1:
            return (count,)
        sizes.append(len({spot[moved[0]] for spot in spots}))
        stride *= sizes[-1]
    return tuple(reversed(sizes)) if stride == count else (count,)


ROWS = 16


class Plan:
    def __init__(self, factors, shapes):
        self.factors = tuple(factors)
        self.strides = [math.prod(factors[i + 1 :]) for i in range(len(factors))]
        live = [a for a in range(len(factors)) if factors[a] > 1]
        live.sort(key=lambda a: (factors[a], -a))
        self.orders = [tuple(live)]
        if len(live) > 1:
            self.orders.append((live[1], live[0], *live[2:]))
        self.live = live
        self.chunks = []
        early = len(live) > 2 and sum(rows // ROWS for rows, _ in shapes) > 6
        for array, (rows, cols) in enumerate(shapes):
            step = ROWS if rows % ROWS == 0 else rows
            for start in range(0, rows, step):
                order = self.orders[len(self.chunks) % len(self.orders)]
                if early and not self.chunks:
                    order = (live[2], live[1], live[0], *live[3:])
                self.chunks.append((array, start, step, cols, order))
        width, rest = len(self.orders), list(range(int(early), len(self.chunks)))
        self.groups = [rest[at : at + width] for at in range(0, len(rest), width)]
        self.early = [0] if early else []
        if early:
            self.groups[2] = [*self.groups[2], 0]

    def scratch(self):
        shapes = []
        for _, _, step, cols, order in self.chunks:
            rest = list(range(len(self.factors)))
            for axis in order:
                rest.remove(axis)
                dims = tuple(self.factors[a] for a in rest)
                shapes.append(pltpu.VMEM((self.factors[axis] - 1, *dims, step, cols), jnp.bfloat16))
                shapes.append(pltpu.VMEM((*dims, step, cols), jnp.bfloat16))
        return shapes


def scatter_kernel(plan, arrays, *refs):
    grads, outs = refs[:arrays], refs[arrays : 2 * arrays]
    bufs, (own_sem, send_sem, recv_sem) = refs[2 * arrays : -3], refs[-3:]
    factors, strides = plan.factors, plan.strides
    me = lax.axis_index("dp")
    spot = [(me // strides[a]) % factors[a] for a in range(len(factors))]
    stages = len(plan.live)

    def peer(axis, hop):
        place = (spot[axis] + hop) % factors[axis]
        return place, me + (place - spot[axis]) * strides[axis]

    barrier = pltpu.get_barrier_semaphore()
    total = 0
    for axis in plan.live:
        for hop in range(1, factors[axis]):
            pl.semaphore_signal(
                barrier,
                inc=1,
                device_id={"dp": peer(axis, hop)[1]},
                device_id_type=pl.DeviceIdType.MESH,
            )
            total += 1
    pl.semaphore_wait(barrier, total)

    base = {axis: 0 for axis in plan.live}
    count = 0
    for axis in plan.live:
        base[axis] = count
        count += factors[axis] - 1

    def view(chunk, stage, place):
        array, start, step, _, order = plan.chunks[chunk]
        axis = order[stage]
        rest = [a for a in range(len(factors)) if a not in order[:stage]]
        index = tuple(place if a == axis else slice(None) for a in rest)
        if stage == 0:
            return grads[array].at[(*index, pl.ds(start, step))]
        return buf(chunk, stage - 1)[1].at[index]

    def buf(chunk, stage):
        at = 2 * (chunk * stages + stage)
        return bufs[at], bufs[at + 1]

    def own_copy(chunk):
        axis = plan.chunks[chunk][4][0]
        return pltpu.make_async_copy(
            view(chunk, 0, spot[axis]), buf(chunk, 0)[1], own_sem.at[chunk]
        )

    def sends(chunk, stage):
        axis = plan.chunks[chunk][4][stage]
        made = []
        for hop in range(1, factors[axis]):
            place, device = peer(axis, hop)
            made.append(
                pltpu.make_async_remote_copy(
                    src_ref=view(chunk, stage, place),
                    dst_ref=buf(chunk, stage)[0].at[hop - 1],
                    send_sem=send_sem.at[chunk, base[axis] + hop - 1],
                    recv_sem=recv_sem.at[chunk, base[axis] + hop - 1],
                    device_id={"dp": device},
                    device_id_type=pl.DeviceIdType.MESH,
                )
            )
        return made

    def launch(chunk, stage):
        for copy in sends(chunk, stage):
            copy.start()
        if stage == 0:
            own_copy(chunk).start()

    def finish(chunk, stage):
        array, start, step, _, order = plan.chunks[chunk]
        axis = order[stage]
        arrived, kept = buf(chunk, stage)
        if stage == 0:
            own_copy(chunk).wait()
        for copy in sends(chunk, stage):
            copy.wait_recv()
        rest = [a for a in range(len(factors)) if a not in order[: stage + 1]]
        dims = [factors[a] for a in rest]

        def add(flat, carry):
            at, left = [], flat
            for size in reversed(dims):
                at.insert(0, left % size)
                left = left // size
            at = tuple(at)
            if stage == 0:
                value = kept[at].astype(jnp.float32) if at else kept[...].astype(jnp.float32)
            else:
                mine, inner = buf(chunk, stage - 1)[1], list(at)
                before = [a for a in range(len(factors)) if a not in order[:stage]]
                inner.insert(before.index(axis), spot[axis])
                value = mine[tuple(inner)].astype(jnp.float32)
            for hop in range(1, factors[axis]):
                value = value + arrived[(hop - 1, *at)].astype(jnp.float32)
            if stage == stages - 1:
                outs[array][pl.ds(start, step), :] = value.reshape(step, -1)
            elif at:
                kept[at] = value.astype(jnp.bfloat16)
            return carry

        blocks = math.prod(dims)
        if blocks == 1:
            add(0, 0)
        else:
            lax.fori_loop(0, blocks, add, 0)

    groups = plan.groups
    ahead = 3
    first = [[c for c in group if c not in plan.early] for group in groups]
    for group in [first[0], plan.early, *first[1:ahead]]:
        for chunk in group:
            launch(chunk, 0)
    for step in range(len(groups) + stages - 1):
        for stage in range(stages):
            if 0 <= step - stage < len(groups):
                for chunk in groups[step - stage]:
                    finish(chunk, stage)
                    if stage + 1 < stages:
                        launch(chunk, stage + 1)
                if stage == 0 and step + ahead < len(groups):
                    for chunk in first[step + ahead]:
                        launch(chunk, 0)
    for chunk in range(len(plan.chunks)):
        for stage in range(stages):
            for copy in sends(chunk, stage):
                copy.wait_send()


def scatter_sum(factors, grads):
    count = math.prod(factors)
    shapes = [(g.shape[0] // count, g.shape[1]) for g in grads]
    plan = Plan(factors, shapes)
    hops = sum(factors[a] - 1 for a in plan.live)
    chunks = len(plan.chunks)
    views = [g.reshape(*factors, *shape) for g, shape in zip(grads, shapes)]
    return pl.pallas_call(
        functools.partial(scatter_kernel, plan, len(grads)),
        out_shape=[jax.ShapeDtypeStruct(shape, jnp.float32) for shape in shapes],
        in_specs=[pl.BlockSpec(memory_space=pl.ANY)] * len(grads),
        out_specs=[pl.BlockSpec(memory_space=pltpu.VMEM)] * len(grads),
        scratch_shapes=plan.scratch()
        + [
            pltpu.SemaphoreType.DMA((chunks,)),
            pltpu.SemaphoreType.DMA((chunks, hops)),
            pltpu.SemaphoreType.DMA((chunks, hops)),
        ],
        compiler_params=pltpu.CompilerParams(
            collective_id=0, has_side_effects=True, vmem_limit_bytes=48 * 1024 * 1024
        ),
    )(*views)


def error_kernel(scale, owner_ref, pred_ref, block_ref, out_ref):
    gap = pred_ref[...] - block_ref[...].astype(jnp.float32)
    out_ref[...] = (gap * scale).astype(out_ref.dtype)


def scaled_error(scale, sample_owner, pred, arrived):
    patches, width = arrived.shape[1:]
    rows = pl.BlockSpec((patches, width), lambda i, owner: (i, 0))
    picked = pl.BlockSpec((None, patches, width), lambda i, owner: (owner[i], 0, 0))
    return pl.pallas_call(
        functools.partial(error_kernel, scale),
        out_shape=jax.ShapeDtypeStruct(pred.shape, jnp.bfloat16),
        grid_spec=pltpu.PrefetchScalarGridSpec(
            num_scalar_prefetch=1,
            grid=(sample_owner.shape[0],),
            in_specs=[rows, picked],
            out_specs=rows,
        ),
        cost_estimate=pl.CostEstimate(
            flops=2 * pred.size, bytes_accessed=8 * pred.size, transcendentals=0
        ),
    )(sample_owner, pred, arrived)


def rows_kernel(left_ref, right_ref, out_ref):
    out_ref[...] = lax.dot_general(
        left_ref[...],
        right_ref[...],
        (((0,), (0,)), ((), ())),
        preferred_element_type=jnp.float32,
    ).astype(out_ref.dtype)


def outer_product(left, right):
    depth, rows = left.shape
    cols = right.shape[1]
    tile = 256 if rows % 256 == 0 else rows
    return pl.pallas_call(
        rows_kernel,
        out_shape=jax.ShapeDtypeStruct((rows, cols), jnp.bfloat16),
        grid=(rows // tile,),
        in_specs=[
            pl.BlockSpec((depth, tile), lambda i: (0, i)),
            pl.BlockSpec((depth, cols), lambda i: (0, 0)),
        ],
        out_specs=pl.BlockSpec((tile, cols), lambda i: (i, 0)),
        cost_estimate=pl.CostEstimate(
            flops=2 * depth * rows * cols,
            bytes_accessed=2 * (depth * rows + depth * cols + rows * cols),
            transcendentals=0,
        ),
    )(left, right)


def per_device(
    factors,
    tokens, sample_owner, sample_slot, teacher_cache, fc_weight, proj_weight, head_weight
):
    devices = lax.axis_size("dp")
    tok_rows = tokens.shape[0]
    loss_scale = 1.0 / math.sqrt(tok_rows * devices)
    owner_table = (sample_owner[:, None] == jnp.arange(devices, dtype=jnp.int32)[None, :]).astype(
        jnp.int32
    )
    request = jnp.sum(owner_table * (sample_slot[:, None] + 1), axis=0)
    asked_slots = lax.all_to_all(request, "dp", split_axis=0, concat_axis=0, tiled=True)
    safe_slots = jnp.maximum(asked_slots - 1, 0)
    normal_in, _ = normalize(tokens)
    normed_in = normal_in.astype(jnp.bfloat16)
    pre_act = jnp.dot(normed_in, fc_weight, preferred_element_type=jnp.float32)
    act_out = gelu_tanh(pre_act).astype(jnp.bfloat16)
    partial_value = jnp.dot(act_out, proj_weight, preferred_element_type=jnp.float32)
    mlp_out = pair_sum(partial_value.astype(jnp.bfloat16))
    hidden = tokens.astype(jnp.float32) + mlp_out
    normal_out, inverse = normalize(hidden)
    normed_out = normal_out.astype(jnp.bfloat16)
    stored = jnp.take(teacher_cache, safe_slots, axis=0, mode="clip")
    arrived = lax.all_to_all(stored, "dp", split_axis=0, concat_axis=0, tiled=True)
    pred = jnp.dot(normed_out, head_weight, preferred_element_type=jnp.float32)
    err_scaled = scaled_error(loss_scale, sample_owner, pred, arrived)
    head_grad = outer_product(normed_out, err_scaled)
    grad_part = jnp.dot(err_scaled, head_weight.T, preferred_element_type=jnp.float32)
    grad_norm = pair_sum(grad_part.astype(jnp.bfloat16))
    grad_hidden = inverse * (
        grad_norm
        - jnp.mean(grad_norm, axis=-1, keepdims=True)
        - normal_out * jnp.mean(grad_norm * normal_out, axis=-1, keepdims=True)
    )
    grad_hidden = grad_hidden.astype(jnp.bfloat16)
    proj_grad = jnp.dot(grad_hidden.T, act_out, preferred_element_type=jnp.float32)
    grad_act = jnp.dot(grad_hidden, proj_weight.T, preferred_element_type=jnp.float32)
    grad_pre = (grad_act * gelu_slope(pre_act)).astype(jnp.bfloat16)
    fc_grad = jnp.dot(normed_in.T, grad_pre, preferred_element_type=jnp.float32)
    head_shard, proj_shard, fc_shard = scatter_sum(
        factors,
        [g.astype(jnp.bfloat16) for g in (head_grad, proj_grad, fc_grad)],
    )
    proj_shard = proj_shard.T
    return (fc_shard, proj_shard, head_shard)


def solution(mesh):
    in_specs = (
        P("dp", None),
        P("dp"),
        P("dp"),
        P("dp", None, "mp"),
        P(None, "mp"),
        P("mp", None),
        P(None, "mp"),
    )
    out_specs = (P("dp", "mp"), P("mp", "dp"), P("dp", "mp"))
    return jax.shard_map(
        functools.partial(per_device, dp_factors(mesh)),
        mesh=mesh, in_specs=in_specs, out_specs=out_specs, check_vma=False
    )
```

```python
import functools
import math

import jax
import jax.numpy as jnp
from jax import lax
from jax.experimental import pallas as pl
from jax.experimental.pallas import tpu as pltpu
from jax.sharding import PartitionSpec as P

gelu_coef = 0.7978845608


def normalize(values):
    values = values.astype(jnp.float32)
    center = jnp.mean(values, axis=-1, keepdims=True)
    spread = jnp.mean((values - center) ** 2, axis=-1, keepdims=True)
    inverse = 1.0 / jnp.sqrt(spread + 1e-06)
    return ((values - center) * inverse, inverse)


def gelu_tanh(values):
    return 0.5 * values * (1.0 + jnp.tanh(gelu_coef * (values + 0.044715 * values**3)))


def gelu_slope(values):
    inner = jnp.tanh(gelu_coef * (values + 0.044715 * values**3))
    return 0.5 * (1.0 + inner) + 0.5 * values * (1.0 - inner * inner) * gelu_coef * (
        1.0 + 3.0 * 0.044715 * values * values
    )


def pair_sum(part):
    size = lax.axis_size("mp")
    total = part.astype(jnp.float32)
    for shift in range(1, size):
        moved = lax.ppermute(part, "mp", [(i, (i + shift) % size) for i in range(size)])
        total = total + moved.astype(jnp.float32)
    return total


def dp_factors(mesh):
    count = mesh.shape["dp"]
    lead = mesh.devices.reshape(count, -1)[:, 0]
    spots = [getattr(device, "coords", None) for device in lead]
    if any(spot is None for spot in spots):
        return (count,)
    sizes, stride = [], 1
    while stride < count:
        moved = [a for a in range(len(spots[0])) if spots[0][a] != spots[stride][a]]
        if len(moved) != 1:
            return (count,)
        sizes.append(len({spot[moved[0]] for spot in spots}))
        stride *= sizes[-1]
    return tuple(reversed(sizes)) if stride == count else (count,)


ROWS = 16


class Plan:
    def __init__(self, factors, shapes):
        self.factors = tuple(factors)
        self.strides = [math.prod(factors[i + 1 :]) for i in range(len(factors))]
        live = [a for a in range(len(factors)) if factors[a] > 1]
        live.sort(key=lambda a: (factors[a], -a))
        self.orders = [tuple(live)]
        if len(live) > 1:
            self.orders.append((live[1], live[0], *live[2:]))
        self.live = live
        self.chunks = []
        early = len(live) > 2 and sum(rows // ROWS for rows, _ in shapes) > 6
        for array, (rows, cols) in enumerate(shapes):
            step = ROWS if rows % ROWS == 0 else rows
            for start in range(0, rows, step):
                order = self.orders[len(self.chunks) % len(self.orders)]
                if early and not self.chunks:
                    order = (live[2], live[1], live[0], *live[3:])
                self.chunks.append((array, start, step, cols, order))
        width, rest = len(self.orders), list(range(int(early), len(self.chunks)))
        self.groups = [rest[at : at + width] for at in range(0, len(rest), width)]
        self.early = [0] if early else []
        if early:
            self.groups[2] = [*self.groups[2], 0]

    def scratch(self):
        shapes = []
        for _, _, step, cols, order in self.chunks:
            rest = list(range(len(self.factors)))
            for axis in order:
                rest.remove(axis)
                dims = tuple(self.factors[a] for a in rest)
                shapes.append(pltpu.VMEM((self.factors[axis] - 1, *dims, step, cols), jnp.bfloat16))
                shapes.append(pltpu.VMEM((*dims, step, cols), jnp.bfloat16))
        return shapes


def scatter_kernel(plan, arrays, *refs):
    grads, outs = refs[:arrays], refs[arrays : 2 * arrays]
    bufs, (own_sem, send_sem, recv_sem) = refs[2 * arrays : -3], refs[-3:]
    factors, strides = plan.factors, plan.strides
    me = lax.axis_index("dp")
    spot = [(me // strides[a]) % factors[a] for a in range(len(factors))]
    stages = len(plan.live)

    def peer(axis, hop):
        place = (spot[axis] + hop) % factors[axis]
        return place, me + (place - spot[axis]) * strides[axis]

    barrier = pltpu.get_barrier_semaphore()
    total = 0
    for axis in plan.live:
        for hop in range(1, factors[axis]):
            pl.semaphore_signal(
                barrier,
                inc=1,
                device_id={"dp": peer(axis, hop)[1]},
                device_id_type=pl.DeviceIdType.MESH,
            )
            total += 1
    pl.semaphore_wait(barrier, total)

    base = {axis: 0 for axis in plan.live}
    count = 0
    for axis in plan.live:
        base[axis] = count
        count += factors[axis] - 1

    def view(chunk, stage, place):
        array, start, step, _, order = plan.chunks[chunk]
        axis = order[stage]
        rest = [a for a in range(len(factors)) if a not in order[:stage]]
        index = tuple(place if a == axis else slice(None) for a in rest)
        if stage == 0:
            return grads[array].at[(*index, pl.ds(start, step))]
        return buf(chunk, stage - 1)[1].at[index]

    def buf(chunk, stage):
        at = 2 * (chunk * stages + stage)
        return bufs[at], bufs[at + 1]

    def own_copy(chunk):
        axis = plan.chunks[chunk][4][0]
        return pltpu.make_async_copy(
            view(chunk, 0, spot[axis]), buf(chunk, 0)[1], own_sem.at[chunk]
        )

    def sends(chunk, stage):
        axis = plan.chunks[chunk][4][stage]
        made = []
        for hop in range(1, factors[axis]):
            place, device = peer(axis, hop)
            made.append(
                pltpu.make_async_remote_copy(
                    src_ref=view(chunk, stage, place),
                    dst_ref=buf(chunk, stage)[0].at[hop - 1],
                    send_sem=send_sem.at[chunk, base[axis] + hop - 1],
                    recv_sem=recv_sem.at[chunk, base[axis] + hop - 1],
                    device_id={"dp": device},
                    device_id_type=pl.DeviceIdType.MESH,
                )
            )
        return made

    def launch(chunk, stage):
        for copy in sends(chunk, stage):
            copy.start()
        if stage == 0:
            own_copy(chunk).start()

    def finish(chunk, stage):
        array, start, step, _, order = plan.chunks[chunk]
        axis = order[stage]
        arrived, kept = buf(chunk, stage)
        if stage == 0:
            own_copy(chunk).wait()
        for copy in sends(chunk, stage):
            copy.wait_recv()
        rest = [a for a in range(len(factors)) if a not in order[: stage + 1]]
        dims = [factors[a] for a in rest]

        def add(flat, carry):
            at, left = [], flat
            for size in reversed(dims):
                at.insert(0, left % size)
                left = left // size
            at = tuple(at)
            if stage == 0:
                value = kept[at].astype(jnp.float32) if at else kept[...].astype(jnp.float32)
            else:
                mine, inner = buf(chunk, stage - 1)[1], list(at)
                before = [a for a in range(len(factors)) if a not in order[:stage]]
                inner.insert(before.index(axis), spot[axis])
                value = mine[tuple(inner)].astype(jnp.float32)
            for hop in range(1, factors[axis]):
                value = value + arrived[(hop - 1, *at)].astype(jnp.float32)
            if stage == stages - 1:
                outs[array][pl.ds(start, step), :] = value.reshape(step, -1)
            elif at:
                kept[at] = value.astype(jnp.bfloat16)
            return carry

        blocks = math.prod(dims)
        if blocks == 1:
            add(0, 0)
        else:
            lax.fori_loop(0, blocks, add, 0)

    groups = plan.groups
    ahead = 2
    for group in [groups[0], plan.early, *groups[1:ahead]]:
        for chunk in group:
            launch(chunk, 0)
    for step in range(len(groups) + stages - 1):
        for stage in range(stages):
            if 0 <= step - stage < len(groups):
                for chunk in groups[step - stage]:
                    finish(chunk, stage)
                    if stage + 1 < stages:
                        launch(chunk, stage + 1)
        if step + ahead < len(groups):
            for chunk in groups[step + ahead]:
                if chunk not in plan.early:
                    launch(chunk, 0)
    for chunk in range(len(plan.chunks)):
        for stage in range(stages):
            for copy in sends(chunk, stage):
                copy.wait_send()


def scatter_sum(factors, grads):
    count = math.prod(factors)
    shapes = [(g.shape[0] // count, g.shape[1]) for g in grads]
    plan = Plan(factors, shapes)
    hops = sum(factors[a] - 1 for a in plan.live)
    chunks = len(plan.chunks)
    views = [g.reshape(*factors, *shape) for g, shape in zip(grads, shapes)]
    return pl.pallas_call(
        functools.partial(scatter_kernel, plan, len(grads)),
        out_shape=[jax.ShapeDtypeStruct(shape, jnp.float32) for shape in shapes],
        in_specs=[pl.BlockSpec(memory_space=pl.ANY)] * len(grads),
        out_specs=[pl.BlockSpec(memory_space=pltpu.VMEM)] * len(grads),
        scratch_shapes=plan.scratch()
        + [
            pltpu.SemaphoreType.DMA((chunks,)),
            pltpu.SemaphoreType.DMA((chunks, hops)),
            pltpu.SemaphoreType.DMA((chunks, hops)),
        ],
        compiler_params=pltpu.CompilerParams(
            collective_id=0, has_side_effects=True, vmem_limit_bytes=48 * 1024 * 1024
        ),
    )(*views)


def error_kernel(scale, owner_ref, pred_ref, block_ref, out_ref):
    gap = pred_ref[...] - block_ref[...].astype(jnp.float32)
    out_ref[...] = (gap * scale).astype(out_ref.dtype)


def scaled_error(scale, sample_owner, pred, arrived):
    patches, width = arrived.shape[1:]
    rows = pl.BlockSpec((patches, width), lambda i, owner: (i, 0))
    picked = pl.BlockSpec((None, patches, width), lambda i, owner: (owner[i], 0, 0))
    return pl.pallas_call(
        functools.partial(error_kernel, scale),
        out_shape=jax.ShapeDtypeStruct(pred.shape, jnp.bfloat16),
        grid_spec=pltpu.PrefetchScalarGridSpec(
            num_scalar_prefetch=1,
            grid=(sample_owner.shape[0],),
            in_specs=[rows, picked],
            out_specs=rows,
        ),
        cost_estimate=pl.CostEstimate(
            flops=2 * pred.size, bytes_accessed=8 * pred.size, transcendentals=0
        ),
    )(sample_owner, pred, arrived)


def rows_kernel(left_ref, right_ref, out_ref):
    out_ref[...] = lax.dot_general(
        left_ref[...],
        right_ref[...],
        (((0,), (0,)), ((), ())),
        preferred_element_type=jnp.float32,
    ).astype(out_ref.dtype)


def outer_product(left, right):
    depth, rows = left.shape
    cols = right.shape[1]
    tile = 256 if rows % 256 == 0 else rows
    return pl.pallas_call(
        rows_kernel,
        out_shape=jax.ShapeDtypeStruct((rows, cols), jnp.bfloat16),
        grid=(rows // tile,),
        in_specs=[
            pl.BlockSpec((depth, tile), lambda i: (0, i)),
            pl.BlockSpec((depth, cols), lambda i: (0, 0)),
        ],
        out_specs=pl.BlockSpec((tile, cols), lambda i: (i, 0)),
        cost_estimate=pl.CostEstimate(
            flops=2 * depth * rows * cols,
            bytes_accessed=2 * (depth * rows + depth * cols + rows * cols),
            transcendentals=0,
        ),
    )(left, right)


def per_device(
    factors,
    tokens, sample_owner, sample_slot, teacher_cache, fc_weight, proj_weight, head_weight
):
    devices = lax.axis_size("dp")
    tok_rows = tokens.shape[0]
    loss_scale = 1.0 / math.sqrt(tok_rows * devices)
    owner_table = (sample_owner[:, None] == jnp.arange(devices, dtype=jnp.int32)[None, :]).astype(
        jnp.int32
    )
    request = jnp.sum(owner_table * (sample_slot[:, None] + 1), axis=0)
    asked_slots = lax.all_to_all(request, "dp", split_axis=0, concat_axis=0, tiled=True)
    safe_slots = jnp.maximum(asked_slots - 1, 0)
    normal_in, _ = normalize(tokens)
    normed_in = normal_in.astype(jnp.bfloat16)
    pre_act = jnp.dot(normed_in, fc_weight, preferred_element_type=jnp.float32)
    act_out = gelu_tanh(pre_act).astype(jnp.bfloat16)
    partial_value = jnp.dot(act_out, proj_weight, preferred_element_type=jnp.float32)
    mlp_out = pair_sum(partial_value.astype(jnp.bfloat16))
    hidden = tokens.astype(jnp.float32) + mlp_out
    normal_out, inverse = normalize(hidden)
    normed_out = normal_out.astype(jnp.bfloat16)
    stored = jnp.take(teacher_cache, safe_slots, axis=0, mode="clip")
    arrived = lax.all_to_all(stored, "dp", split_axis=0, concat_axis=0, tiled=True)
    pred = jnp.dot(normed_out, head_weight, preferred_element_type=jnp.float32)
    err_scaled = scaled_error(loss_scale, sample_owner, pred, arrived)
    head_grad = outer_product(normed_out, err_scaled)
    grad_part = jnp.dot(err_scaled, head_weight.T, preferred_element_type=jnp.float32)
    grad_norm = pair_sum(grad_part.astype(jnp.bfloat16))
    grad_hidden = inverse * (
        grad_norm
        - jnp.mean(grad_norm, axis=-1, keepdims=True)
        - normal_out * jnp.mean(grad_norm * normal_out, axis=-1, keepdims=True)
    )
    grad_hidden = grad_hidden.astype(jnp.bfloat16)
    proj_grad = jnp.dot(grad_hidden.T, act_out, preferred_element_type=jnp.float32)
    grad_act = jnp.dot(grad_hidden, proj_weight.T, preferred_element_type=jnp.float32)
    grad_pre = (grad_act * gelu_slope(pre_act)).astype(jnp.bfloat16)
    fc_grad = jnp.dot(normed_in.T, grad_pre, preferred_element_type=jnp.float32)
    head_shard, proj_shard, fc_shard = scatter_sum(
        factors,
        [g.astype(jnp.bfloat16) for g in (head_grad, proj_grad, fc_grad)],
    )
    proj_shard = proj_shard.T
    return (fc_shard, proj_shard, head_shard)


def solution(mesh):
    in_specs = (
        P("dp", None),
        P("dp"),
        P("dp"),
        P("dp", None, "mp"),
        P(None, "mp"),
        P("mp", None),
        P(None, "mp"),
    )
    out_specs = (P("dp", "mp"), P("mp", "dp"), P("dp", "mp"))
    return jax.shard_map(
        functools.partial(per_device, dp_factors(mesh)),
        mesh=mesh, in_specs=in_specs, out_specs=out_specs, check_vma=False
    )
```
